32 devices in a mesh: dp: 4 (over y, core), mp: 8 (over z, x).
Axes of the slice: x: 2, y: 2, z: 4, core: 2. Of those that a mesh axis runs over, the one named last changes fastest.
Arguments:
- tokens: bfloat16 [32, 256, 768], P(('dp', 'mp')), may hold values from -6 to 6
- lengths: int32 [32], P(('dp', 'mp')), may hold values from 64 to 256, as said below
- grad_output: bfloat16 [32, 256, 768], P(('dp', 'mp')), may hold values from -6 to 6
- w_query: bfloat16 [768, 768], P('mp'), may hold values from -0.21875 to 0.21875
- b_query: bfloat16 [768], P('mp'), may hold values from -1.75 to 1.75
- w_key: bfloat16 [768, 768], P('mp'), may hold values from -0.21875 to 0.21875
- b_key: bfloat16 [768], P('mp'), may hold values from -1.75 to 1.75
- w_value: bfloat16 [768, 768], P('mp'), may hold values from -0.21875 to 0.21875
- b_value: bfloat16 [768], P('mp'), may hold values from -1.75 to 1.75
- w_output: bfloat16 [768, 768], P('mp'), may hold values from -0.875 to 0.875
- b_output: bfloat16 [768], P('mp'), may hold values from -1.75 to 1.75
- first_gain: bfloat16 [768], P('mp'), may hold values from 0.099609375 to 1.8984375
- first_bias: bfloat16 [768], P('mp'), may hold values from -1.75 to 1.75
- w_inner: bfloat16 [768, 3072], P('mp'), may hold values from -0.21875 to 0.21875
- b_inner: bfloat16 [3072], P('mp'), may hold values from -1.75 to 1.75
- w_outer: bfloat16 [3072, 768], P('mp'), may hold values from -0.109375 to 0.109375
- b_outer: bfloat16 [768], P('mp'), may hold values from -1.75 to 1.75
- second_gain: bfloat16 [768], P('mp'), may hold values from 0.099609375 to 1.8984375
- second_bias: bfloat16 [768], P('mp'), may hold values from -1.75 to 1.75
- relative_embed: bfloat16 [512, 768], P('mp'), may hold values from -6 to 6
Outputs:
- layer_out: bfloat16 [32, 256, 768], P(('dp', 'mp'))
- grad_input: bfloat16 [32, 256, 768], P(('dp', 'mp'))
- grad_w_query: float32 [768, 768], P('mp')
- grad_b_query: float32 [768], P('mp')
- grad_w_key: float32 [768, 768], P('mp')
- grad_b_key: float32 [768], P('mp')
- grad_w_value: float32 [768, 768], P('mp')
- grad_b_value: float32 [768], P('mp')
- grad_w_output: float32 [768, 768], P('mp')
- grad_b_output: float32 [768], P('mp')
- grad_first_gain: float32 [768], P('mp')
- grad_first_bias: float32 [768], P('mp')
- grad_w_inner: float32 [768, 3072], P('mp')
- grad_b_inner: float32 [3072], P('mp')
- grad_w_outer: float32 [3072, 768], P('mp')
- grad_b_outer: float32 [768], P('mp')
- grad_second_gain: float32 [768], P('mp')
- grad_second_bias: float32 [768], P('mp')
- grad_relative_embed: float32 [512, 768], P('mp')
The draws below stay inside these ranges and needn't reach their ends.
Inputs may be any that keep to these rules, and one draw needn't show every extreme that they name: `lengths`: each row's sequence has its length from 64 to 256; at least one row has 256.
All inputs are finite; a program needn't handle non-finite values.
Results may differ from the reference program's by a relative error of at most 0.025.
Values may be sent and summed in bfloat16 or wider, within the bound.
No kernel may reach another device: no remote copies, remote signals or barrier semaphores. Data moves between devices by JAX's collectives and lax.ppermute only.
A program may use at most 192 MiB of HBM per device.

```python
import math
import jax
import jax.numpy as jnp
from jax import lax

D = 768
HEADS = 12
HEAD_DIM = 64
FF = 3072
SPAN = 256
SLOTS = 256
MIN_LEN = 64
ROWS = 32


def draw_lengths(key, part):
    doubling_key, extra_key, choose_key = jax.random.split(jax.random.fold_in(key, 7), 3)
    top_level = (SLOTS // MIN_LEN).bit_length()
    doubling = jax.random.randint(doubling_key, (ROWS,), 0, top_level + 1)
    lower_end = jnp.left_shift(jnp.int32(MIN_LEN), doubling)
    extra_rows = jax.random.randint(extra_key, (ROWS,), 0, lower_end)
    drawn = jnp.minimum(lower_end + extra_rows, SLOTS)
    longest_row = jax.random.randint(choose_key, (), 0, ROWS)
    return jnp.where(jnp.arange(ROWS, dtype=jnp.int32) == longest_row, SLOTS, drawn).astype(jnp.int32)


def shard_levels(own_key, shape, cuts, low, largest):
    loudness, own = 1.0, jax.random.fold_in(own_key, 6)
    for axis_at, blocks in cuts:
        steps = jnp.exp(jax.random.uniform(jax.random.fold_in(own, axis_at), (blocks,), jnp.float32, low / len(cuts), largest / len(cuts)))
        loudness = loudness * jnp.repeat(steps, shape[axis_at] // blocks).reshape([-1 if axis == axis_at else 1 for axis in range(len(shape))])
    return loudness


def normal_values(rng, extent, scale, most, cuts=(), kind=jnp.bfloat16):
    entries = scale * jax.random.normal(rng, extent, jnp.float32)
    if cuts:
        entries = entries * shard_levels(rng, extent, cuts, -0.22, 0.18)
    return jnp.clip(entries, -most, most).astype(kind)


def setup_inputs(seed: int = 0) -> dict:
    key_of = jax.random.split(jax.random.key(seed), 21)
    return {
        "tokens": normal_values(key_of[0], (ROWS, SLOTS, D), 1.0, 6.0, ((0, 32),)),
        "lengths": draw_lengths(jax.random.fold_in(key_of[20], 71), 0),
        "grad_output": normal_values(key_of[2], (ROWS, SLOTS, D), 1.0, 6.0, ((0, 32),)),
        "w_query": normal_values(key_of[3], (D, D), D ** -0.5, 0.21875, ((0, 8),)),
        "b_query": normal_values(key_of[4], (D,), 0.3, 1.75, ((0, 8),)),
        "w_key": normal_values(key_of[5], (D, D), D ** -0.5, 0.21875, ((0, 8),)),
        "b_key": normal_values(key_of[6], (D,), 0.3, 1.75, ((0, 8),)),
        "w_value": normal_values(key_of[7], (D, D), D ** -0.5, 0.21875, ((0, 8),)),
        "b_value": normal_values(key_of[8], (D,), 0.3, 1.75, ((0, 8),)),
        "w_output": normal_values(key_of[9], (D, D), (D // 16) ** -0.5, 0.875, ((0, 8),)),
        "b_output": normal_values(key_of[10], (D,), 0.3, 1.75, ((0, 8),)),
        "first_gain": jnp.clip(1.0 + 0.18 * jax.random.normal(key_of[11], (D,), jnp.float32), 0.099609375, 1.8984375).astype(jnp.bfloat16),
        "first_bias": normal_values(key_of[12], (D,), 0.3, 1.75, ((0, 8),)),
        "w_inner": normal_values(key_of[13], (D, FF), D ** -0.5, 0.21875, ((0, 8),)),
        "b_inner": normal_values(key_of[14], (FF,), 0.3, 1.75, ((0, 8),)),
        "w_outer": normal_values(key_of[15], (FF, D), FF ** -0.5, 0.109375, ((0, 8),)),
        "b_outer": normal_values(key_of[16], (D,), 0.3, 1.75, ((0, 8),)),
        "second_gain": jnp.clip(1.0 + 0.18 * jax.random.normal(key_of[17], (D,), jnp.float32), 0.099609375, 1.8984375).astype(jnp.bfloat16),
        "second_bias": normal_values(key_of[18], (D,), 0.3, 1.75, ((0, 8),)),
        "relative_embed": normal_values(key_of[19], (2 * SPAN, D), 1.0, 6.0, ((0, 8),)),
    }


EPS = 1e-06
HIGH = lax.Precision.HIGHEST

@jax.custom_vjp
def low(v):
    return lax.optimization_barrier(v.astype(jnp.bfloat16)).astype(jnp.float32)

@jax.custom_vjp
def low_back(v):
    return v

def low_keep(v):
    return (low(v), None)

def low_pass(kept, grad):
    return (grad,)

def back_keep(v):
    return (v, None)

def back_low(kept, grad):
    return (low(grad),)
low.defvjp(low_keep, low_pass)
low_back.defvjp(back_keep, back_low)

def bucket_table(slot_count, span_width):
    places = jnp.arange(slot_count, dtype=jnp.int32)
    return jnp.clip(places[:, None] - places[None, :], -span_width, span_width - 1) + span_width

def layer_norm(hidden, norm_gain, norm_shift):
    centred = hidden - lax.optimization_barrier(jnp.mean(hidden, axis=-1, keepdims=True))
    spread = lax.optimization_barrier(jnp.mean(centred * centred, axis=-1, keepdims=True))
    return centred * lax.rsqrt(spread + EPS) * norm_gain + norm_shift

def relative_gather(score_table, buckets):
    bucket_index = jnp.broadcast_to(buckets, (score_table.shape[0],) + buckets.shape)
    return jnp.take_along_axis(score_table, bucket_index, axis=2)

def split_heads(matrix):
    return matrix.reshape(matrix.shape[0], HEADS, HEAD_DIM).transpose(1, 0, 2)

def row_forward(params, rel_keys, rel_queries, row_input, length):
    w_query, b_query, w_key, b_key, w_value, b_value, w_output, b_output, first_gain, first_bias, w_inner, b_inner, w_outer, b_outer, second_gain, second_bias = params
    score_scale = 1.0 / math.sqrt(3.0 * HEAD_DIM)
    valid_keys = jnp.arange(SLOTS, dtype=jnp.int32) < length
    buckets = bucket_table(SLOTS, SPAN)
    queries = low(low_back(jnp.dot(row_input, w_query, precision=HIGH) + b_query))
    key_rows = low(low_back(jnp.dot(row_input, w_key, precision=HIGH) + b_key))
    value_rows = low(low_back(jnp.dot(row_input, w_value, precision=HIGH) + b_value))
    head_queries = split_heads(queries)
    head_keys = split_heads(key_rows)
    head_values = split_heads(value_rows)
    head_rel_keys = split_heads(rel_keys)
    head_rel_queries = split_heads(rel_queries)
    content = jnp.einsum('hqd,hkd->hqk', head_queries, head_keys, precision=HIGH)
    query_table = low_back(jnp.einsum('hqd,hrd->hqr', head_queries, head_rel_keys, precision=HIGH))
    key_table = low_back(jnp.einsum('hkd,hrd->hkr', head_keys, head_rel_queries, precision=HIGH))
    scores = low_back((content + relative_gather(query_table, buckets) + jnp.swapaxes(relative_gather(key_table, buckets), 1, 2)) * score_scale)
    scores = jnp.where(valid_keys[None, None, :], scores, -1000000000.0)
    row_max = lax.optimization_barrier(jnp.max(scores, axis=-1, keepdims=True))
    exponent = jnp.exp(scores - row_max)
    soft_weights = exponent / lax.optimization_barrier(jnp.sum(exponent, axis=-1, keepdims=True))
    context = jnp.einsum('hqk,hkd->hqd', low(soft_weights), head_values, precision=HIGH)
    context = low(low_back(context.transpose(1, 0, 2).reshape(SLOTS, D)))
    attended = row_input + low_back(jnp.dot(context, w_output, precision=HIGH) + b_output)
    first_out = layer_norm(attended, first_gain, first_bias)
    inner_pre = low_back(jnp.dot(low(first_out), w_inner, precision=HIGH) + b_inner)
    active = low(jax.nn.gelu(inner_pre, approximate=False))
    second_in = first_out + low_back(jnp.dot(active, w_outer, precision=HIGH) + b_outer)
    return layer_norm(second_in, second_gain, second_bias) * valid_keys.astype(jnp.float32)[:, None]

def forward(tokens, w_query, b_query, w_key, b_key, w_value, b_value, w_output, b_output, first_gain, first_bias, w_inner, b_inner, w_outer, b_outer, second_gain, second_bias, relative_embed, lengths):
    params = (w_query, b_query, w_key, b_key, w_value, b_value, w_output, b_output, first_gain, first_bias, w_inner, b_inner, w_outer, b_outer, second_gain, second_bias)
    rel_keys = low(jnp.dot(relative_embed, w_key, precision=HIGH) + b_key)
    rel_queries = low(jnp.dot(relative_embed, w_query, precision=HIGH) + b_query)

    def group_fn(group_items):
        group_rows, group_lengths = group_items
        return jax.vmap(lambda one_row, one_len: row_forward(params, rel_keys, rel_queries, one_row, one_len))(group_rows, group_lengths)
    outputs = lax.map(jax.checkpoint(group_fn), (tokens.reshape(ROWS // 4, 4, SLOTS, D), lengths.reshape(ROWS // 4, 4)))
    return outputs.reshape(ROWS, SLOTS, D)

def reference(tokens, lengths, grad_output, w_query, b_query, w_key, b_key, w_value, b_value, w_output, b_output, first_gain, first_bias, w_inner, b_inner, w_outer, b_outer, second_gain, second_bias, relative_embed):
    floats = (tokens, w_query, b_query, w_key, b_key, w_value, b_value, w_output, b_output, first_gain, first_bias, w_inner, b_inner, w_outer, b_outer, second_gain, second_bias, relative_embed)
    floats = tuple((operand.astype(jnp.float32) for operand in floats))

    def wrapped(*operands):
        return forward(*operands, lengths)
    layer_value, pullback = jax.vjp(wrapped, *floats)
    gradients = pullback(grad_output.astype(jnp.float32))
    row_share = 1.0 / ROWS
    return (layer_value.astype(jnp.bfloat16), gradients[0].astype(jnp.bfloat16), gradients[1] * row_share, gradients[2] * row_share, gradients[3] * row_share, gradients[4] * row_share, gradients[5] * row_share, gradients[6] * row_share, gradients[7] * row_share, gradients[8] * row_share, gradients[9] * row_share, gradients[10] * row_share, gradients[11] * row_share, gradients[12] * row_share, gradients[13] * row_share, gradients[14] * row_share, gradients[15] * row_share, gradients[16] * row_share, gradients[17] * row_share)
```

```python
import functools
import math

import jax
import jax.numpy as jnp
from jax import lax
from jax.experimental import pallas as pl
from jax.experimental.pallas import tpu as pltpu
from jax.sharding import PartitionSpec as P

D = 768
HEADS = 12
HEAD_DIM = 64
PAIRS = HEADS // 2
GROUPS = 4
HALF = D // 2
SMALL = 16
EPS = 1e-06
F32 = jnp.float32
BF16 = jnp.bfloat16
VMEM_LIMIT = 58 * 1024 * 1024


ANY = pl.BlockSpec(memory_space=pl.ANY)
VM = pl.BlockSpec(memory_space=pltpu.VMEM)
SM = pl.BlockSpec(memory_space=pltpu.SMEM)


def dot(a, b):
    return jnp.dot(a, b, preferred_element_type=F32)


def dot_nt(a, b):
    return lax.dot_general(a, b, (((1,), (1,)), ((), ())), preferred_element_type=F32)


def dot_tn(a, b):
    return lax.dot_general(a, b, (((0,), (0,)), ((), ())), preferred_element_type=F32)


def flip_matrix(size):
    row = lax.broadcasted_iota(jnp.int32, (size, size), 0)
    col = lax.broadcasted_iota(jnp.int32, (size, size), 1)
    return jnp.where(row + col == size - 1, 1.0, 0.0).astype(BF16)


def cost(flops, moved, transcendentals=0):
    return pl.CostEstimate(flops=flops, bytes_accessed=moved, transcendentals=transcendentals)


def params(**kwargs):
    return pltpu.CompilerParams(vmem_limit_bytes=VMEM_LIMIT, **kwargs)


def start(src, dst, sem):
    pltpu.make_async_copy(src, dst, sem).start()


def wait_whole(buf, sem):
    pltpu.make_async_copy(buf, buf, sem).wait()


def row_pick(unit):
    row = lax.broadcasted_iota(jnp.int32, (SMALL, 128), 0)
    col = lax.broadcasted_iota(jnp.int32, (SMALL, 128), 1)
    inner = (2 * (row - 9) + unit // 4) * SMALL + 9 + unit % 4
    target = jnp.where(row < 9, unit * SMALL + row, jnp.where(row < 13, inner, -1))
    return jnp.where(col == target, 1.0, 0.0).astype(BF16)


def lane_place(unit, width):
    src = lax.broadcasted_iota(jnp.int32, (128, D), 0)
    dst = lax.broadcasted_iota(jnp.int32, (128, D), 1)
    return jnp.where((dst == unit * width + src) & (src < width), 1.0, 0.0).astype(BF16)


def spread_small(blocks, width):
    full = jnp.zeros((SMALL, D), F32)
    for unit in range(8):
        picked = dot(row_pick(unit), blocks).astype(BF16)
        full = full + dot(picked, lane_place(unit, width))
    return full


def cut_small(full, width):
    low = full.astype(BF16)
    blocks = jnp.zeros((128, 128), F32)
    for unit in range(8):
        lanes = dot_nt(low, lane_place(unit, width)).astype(BF16)
        blocks = blocks + dot_tn(row_pick(unit), lanes)
    return blocks.astype(BF16)


def project_kernel(rows, pieces, meta, *refs):
    d, e = rows
    if pieces:
        own, others = refs[0], refs[1 : 1 + len(pieces)]
        at = 1 + len(pieces)
    else:
        full_w, full_rel, full_small = refs[:3]
        at = 3
    tok, qkv, wout, rel_out, rk_rev, rq_rev, rq, small, wbuf, relbuf, smbuf, sems = refs[at:]
    if pieces:
        shard = meta[0]

        def place(src, s, col, width, src_col):
            for p in range(3):
                start(
                    src.at[pl.ds(p * d, d), pl.ds(src_col, width)],
                    wbuf.at[p, pl.ds(pl.multiple_of(s * d, 8), d), pl.ds(col, width)],
                    sems.at[0],
                )
            start(
                src.at[pl.ds(3 * d, e), pl.ds(src_col, width)],
                relbuf.at[pl.ds(pl.multiple_of(s * e, 8), e), pl.ds(col, width)],
                sems.at[1],
            )

        def place_small(src, s):
            start(
                src.at[pl.ds(3 * d + e, SMALL), pl.ds(0, 128)],
                smbuf.at[pl.ds(pl.multiple_of(s * SMALL, SMALL), SMALL), :],
                sems.at[2],
            )

        place(own, shard, 0, D, 0)
        place_small(own, shard)
        for (slot, other), ref in zip(pieces, others):
            s = meta[slot]
            half = meta[8]
            col = pl.multiple_of((1 - half if other else half) * HALF, 128)
            place(ref, s, col, HALF, 0)
            if not other:
                place_small(ref, s)
        wait_whole(smbuf, sems.at[2])
        small[...] = spread_small(smbuf[...], d)
        wait_whole(relbuf, sems.at[1])
        wait_whole(wbuf, sems.at[0])
    else:
        start(full_w, wbuf, sems.at[0])
        start(full_rel, relbuf, sems.at[1])
        small[...] = full_small[...]
        wait_whole(relbuf, sems.at[1])
        wait_whole(wbuf, sems.at[0])
    pltpu.make_async_copy(wbuf, wout, sems.at[0]).start()
    pltpu.make_async_copy(relbuf, rel_out, sems.at[1]).start()

    def one(p, _):
        bias = small[pl.ds(p, 1), :]
        qkv[p] = (dot(tok[...], wbuf[p]) + bias).astype(BF16)
        return 0

    lax.fori_loop(0, 3, one, 0)
    flip = flip_matrix(relbuf.shape[0])
    rel = relbuf[...]
    rel_k = (dot(rel, wbuf[1]) + small[pl.ds(1, 1), :]).astype(BF16)
    rk_rev[...] = dot(flip, rel_k).astype(BF16)
    rel_q = (dot(rel, wbuf[0]) + small[pl.ds(0, 1), :]).astype(BF16)
    rq[...] = rel_q
    rq_rev[...] = dot(flip, rel_q).astype(BF16)
    pltpu.make_async_copy(wbuf, wout, sems.at[0]).wait()
    pltpu.make_async_copy(relbuf, rel_out, sems.at[1]).wait()


def project(rows, pieces, meta, sources, tok):
    table = jax.ShapeDtypeStruct((2 * 256, D), BF16)
    slots = tok.shape[0]
    in_specs = [SM] + [ANY] * len(sources) + [VM]
    if not pieces:
        in_specs[3] = VM
    return pl.pallas_call(
        functools.partial(project_kernel, rows, pieces),
        in_specs=in_specs,
        out_specs=[VM, ANY, ANY, VM, VM, VM, VM],
        out_shape=[
            jax.ShapeDtypeStruct((3, slots, D), BF16),
            jax.ShapeDtypeStruct((3, D, D), BF16),
            table,
            table,
            table,
            table,
            jax.ShapeDtypeStruct((SMALL, D), F32),
        ],
        scratch_shapes=[
            pltpu.VMEM((3, D, D), BF16),
            pltpu.VMEM((512, D), BF16),
            pltpu.VMEM((128, 128), BF16),
            pltpu.SemaphoreType.DMA((3,)),
        ],
        compiler_params=params(),
        cost_estimate=cost(2 * D * D * (3 * 256 + 2 * 512), 12 * 2**20),
        name="project",
    )(meta, *sources, tok)


def pair_mask(which):
    lane = lax.broadcasted_iota(jnp.int32, (1, 2 * HEAD_DIM), 1)
    return jnp.where(lane // HEAD_DIM == which, 1.0, 0.0).astype(BF16)


def attend_kernel(length, q, k, v, rk_rev, rq_rev, ctx, probs):
    slots = q.shape[1]
    scale = 1.0 / math.sqrt(3.0 * HEAD_DIM)
    valid = lax.broadcasted_iota(jnp.int32, (1, slots), 1) < length[0]
    total = None
    for which in range(2):
        mask = pair_mask(which)
        qh = q[0] * mask
        kh = k[0] * mask
        score = dot_nt(qh, k[0])
        by_query = pltpu.roll(dot_nt(qh, rk_rev[...]), slots + 1, 1, stride=1, stride_axis=0)
        by_key = pltpu.roll(dot_nt(kh, rq_rev[...]), slots + 1, 1, stride=1, stride_axis=0)
        score = (score + by_query[:, :slots] + by_key[:, :slots].T) * scale
        score = jnp.where(valid, score, -1000000000.0)
        top = jnp.max(score, axis=-1, keepdims=True)
        exponent = jnp.exp(score - top)
        soft = exponent / jnp.sum(exponent, axis=-1, keepdims=True)
        probs[which] = soft
        part = dot(soft.astype(BF16), v[0] * mask)
        total = part if total is None else total + part
    ctx[...] = total.astype(BF16)


def attend(length, qkv, rk_rev, rq_rev, first, count):
    slots = qkv.shape[1]
    width = 2 * HEAD_DIM

    def part(p):
        return pl.BlockSpec((1, slots, width), lambda h: (p, 0, first + h))

    table = pl.BlockSpec((2 * slots, width), lambda h: (0, first + h))
    return pl.pallas_call(
        attend_kernel,
        grid=(count,),
        in_specs=[SM, part(0), part(1), part(2), table, table],
        out_specs=[
            pl.BlockSpec((slots, width), lambda h: (0, h)),
            pl.BlockSpec((2, slots, slots), lambda h: (h, 0, 0)),
        ],
        out_shape=[
            jax.ShapeDtypeStruct((slots, count * width), BF16),
            jax.ShapeDtypeStruct((2 * count, slots, slots), F32),
        ],
        compiler_params=params(),
        cost_estimate=cost(count * 2 * 6 * 2 * slots * slots * 128, count * 2**20),
        name="attend",
    )(length, qkv, qkv, qkv, rk_rev, rq_rev)


def attend_back_kernel(q, k, v, rk_rev, rq, gctx, probs, dq, dk, dv, drk_rev, drq):
    slots = q.shape[1]
    scale = 1.0 / math.sqrt(3.0 * HEAD_DIM)
    flip = flip_matrix(slots)
    blank = jnp.zeros((slots, slots), F32)
    q_flip = dot(flip, q[0]).astype(BF16)
    grads = [None] * 5
    for which in range(2):
        mask = pair_mask(which)
        gh = gctx[...] * mask
        soft = probs[which]
        grad_soft = dot_nt(gh, v[0])
        inner = jnp.sum(soft * grad_soft, axis=-1, keepdims=True)
        grad_score = (soft * (grad_soft - inner)).astype(BF16)
        flipped = dot(flip, grad_score)
        turned = flipped.T
        by_query = pltpu.roll(
            jnp.concatenate([flipped, blank], axis=1), 0, 1, stride=1, stride_axis=0
        )
        by_key = pltpu.roll(
            jnp.concatenate([turned, blank], axis=1), 1, 1, stride=1, stride_axis=0
        )
        by_query = (by_query * scale).astype(BF16)
        by_key = (by_key * scale).astype(BF16)
        kh = k[0] * mask
        qh = q_flip * mask
        news = (
            dot(flipped.astype(BF16), kh) * scale + dot(by_query, rk_rev[...] * mask),
            dot(turned.astype(BF16), qh) * scale + dot(by_key, rq[...] * mask),
            dot_tn(soft.astype(BF16), gh),
            dot_tn(by_query, qh),
            dot_tn(by_key, kh),
        )
        grads = [new if old is None else old + new for old, new in zip(grads, news)]
    dq[...] = dot(flip, grads[0].astype(BF16)).astype(BF16)
    dk[...] = grads[1].astype(BF16)
    dv[...] = grads[2].astype(BF16)
    drk_rev[...] = grads[3].astype(BF16)
    drq[...] = grads[4].astype(BF16)


def attend_back(qkv, rk_rev, rq, gctx, probs, first, count):
    slots = qkv.shape[1]
    width = 2 * HEAD_DIM

    def part(p):
        return pl.BlockSpec((1, slots, width), lambda h: (p, 0, first + h))

    table = pl.BlockSpec((2 * slots, width), lambda h: (0, first + h))
    row_out = pl.BlockSpec((slots, width), lambda h: (0, h))
    table_out = pl.BlockSpec((2 * slots, width), lambda h: (0, h))
    row_shape = jax.ShapeDtypeStruct((slots, count * width), BF16)
    table_shape = jax.ShapeDtypeStruct((2 * slots, count * width), BF16)
    return pl.pallas_call(
        attend_back_kernel,
        grid=(count,),
        in_specs=[
            part(0),
            part(1),
            part(2),
            table,
            table,
            pl.BlockSpec((slots, width), lambda h: (0, first + h)),
            pl.BlockSpec((2, slots, slots), lambda h: (h, 0, 0)),
        ],
        out_specs=[row_out, row_out, row_out, table_out, table_out],
        out_shape=[row_shape, row_shape, row_shape, table_shape, table_shape],
        compiler_params=params(),
        cost_estimate=cost(count * 2 * 13 * 2 * slots * slots * 128, count * 2**20),
        name="attend_back",
    )(qkv, qkv, qkv, rk_rev, rq, gctx, probs)


def centre(value):
    return value - jnp.mean(value, axis=-1, keepdims=True)


def norm_back(grad, normed, inverse, gain):
    scaled = grad * gain
    mean_one = jnp.mean(scaled, axis=-1, keepdims=True)
    mean_two = jnp.mean(scaled * normed, axis=-1, keepdims=True)
    return inverse * (scaled - mean_one - normed * mean_two)


def column_sum(value):
    return jnp.sum(value, axis=0, keepdims=True)


def middle_kernel(rows, pieces, parts, meta, length, *refs):
    d, f = rows
    if pieces:
        w_outer, w_inner, w_output = refs[:3]
        others = refs[3 : 3 + len(pieces)]
        at = 3 + len(pieces)
    else:
        w_outer, w_inner, w_output = refs[:3]
        at = 3
    ctx_parts = refs[at : at + parts]
    tok, gout, small = refs[at + parts : at + parts + 3]
    at = at + parts + 3
    layer, gatt, gctx, gsmall = refs[at : at + 4]
    outs = refs[at + 4 : -13]
    wf, wo, gf, go, act, slope, first, normed1, acc, low, wide, ctxbuf, sems = refs[-13:]
    ff = wf.shape[0] // 2
    slots = tok.shape[0]

    if pieces:
        shard = meta[0]
        half = meta[8]
        kind = meta[9]
        block = f // GROUPS

        def block_row(t, s, b):
            return jnp.where(t == 0, s * f + b * block, ff + b * D + s * d)

        start(w_output, wo.at[pl.ds(pl.multiple_of(shard * d, 8), d), :], sems.at[1])
        start(w_outer, wf.at[pl.ds(pl.multiple_of(shard * f, 8), f), :], sems.at[0])
        for b in range(GROUPS):
            start(
                w_inner.at[:, pl.ds(b * D, D)],
                wf.at[pl.ds(pl.multiple_of(ff + b * D + shard * d, 8), d), :],
                sems.at[0],
            )
        for (slot, other_half, other_kind), ref in zip(pieces, others):
            s = meta[slot]
            h = 1 - half if other_half else half
            t = 1 - kind if other_kind else kind
            col = pl.multiple_of(h * HALF, 128)
            for b in range(GROUPS):
                row = pl.multiple_of(block_row(t, s, b), 8)
                start(
                    ref.at[pl.ds(b * block, block), :],
                    wf.at[pl.ds(row, block), pl.ds(col, HALF)],
                    sems.at[0],
                )
            row = pl.multiple_of(s * d + t * (d // 2), 8)
            start(
                ref.at[pl.ds(f, d // 2), :],
                wo.at[pl.ds(row, d // 2), pl.ds(col, HALF)],
                sems.at[1],
            )
    else:
        start(w_output, wo, sems.at[1])
        start(w_outer, wf.at[pl.ds(0, ff), :], sems.at[0])
        for b in range(GROUPS):
            start(w_inner.at[:, pl.ds(b * D, D)], wf.at[pl.ds(ff + b * D, D), :], sems.at[0])

    width = ctx_parts[0].shape[1]
    for i, part in enumerate(ctx_parts):
        ctxbuf[:, i * width : (i + 1) * width] = part[...]
    wait_whole(wo, sems.at[1])
    attended = tok[...].astype(F32) + (dot(ctxbuf[...], wo[...]) + small[3:4, :])
    centred = centre(attended)
    inverse1 = lax.rsqrt(jnp.mean(centred * centred, axis=-1, keepdims=True) + EPS)
    n1 = centred * inverse1
    normed1[...] = n1
    first_out = n1 * small[4:5, :] + small[5:6, :]
    first[...] = first_out
    low[...] = first_out.astype(BF16)
    acc[...] = first_out + small[6:7, :]
    wait_whole(wf, sems.at[0])

    def forward(g, _):
        pre = dot(low[...], wf[pl.ds(ff + g * D, D), :]) + small[pl.ds(9 + g, 1), :]
        cdf = 0.5 + 0.5 * lax.erf(pre * math.sqrt(0.5))
        act[g] = (pre * cdf).astype(BF16)
        slope[g] = cdf + pre * (jnp.exp(-0.5 * pre * pre) * (1.0 / math.sqrt(2.0 * math.pi)))
        acc[...] += dot(act[g], wf[pl.ds(g * D, D), :])
        return 0

    lax.fori_loop(0, GROUPS, forward, 0)
    column = lax.broadcasted_iota(jnp.int32, (slots, 1), 0)
    mask = jnp.where(column < length[0], 1.0, 0.0)
    centred = centre(acc[...])
    inverse2 = lax.rsqrt(jnp.mean(centred * centred, axis=-1, keepdims=True) + EPS)
    n2 = centred * inverse2
    gain2 = small[7:8, :]
    layer[...] = ((n2 * gain2 + small[8:9, :]) * mask).astype(BF16)
    grad_layer = gout[...].astype(F32) * mask
    gsmall[...] = jnp.zeros(gsmall.shape, F32)
    gsmall[7:8, :] = column_sum(grad_layer * n2)
    gsmall[8:9, :] = column_sum(grad_layer)
    grad_second = norm_back(grad_layer, n2, inverse2, gain2)
    wide[...] = grad_second.astype(BF16)
    gsmall[6:7, :] = column_sum(wide[...].astype(F32))
    acc[...] = grad_second

    def backward(g, _):
        gf[pl.ds(g * D, D), :] = dot_tn(act[g], wide[...]).astype(BF16)
        grad_act = dot_nt(wide[...], wf[pl.ds(g * D, D), :])
        grad_pre = (slope[g] * grad_act).astype(BF16)
        gsmall[pl.ds(9 + g, 1), :] = column_sum(grad_pre.astype(F32))
        gf[pl.ds(ff + g * D, D), :] = dot_tn(low[...], grad_pre).astype(BF16)
        acc[...] += dot_nt(grad_pre, wf[pl.ds(ff + g * D, D), :])
        return 0

    lax.fori_loop(0, GROUPS, backward, 0)
    grad_first = acc[...]
    n1 = normed1[...]
    gsmall[4:5, :] = column_sum(grad_first * n1)
    gsmall[5:6, :] = column_sum(grad_first)
    grad_attended = norm_back(grad_first, n1, inverse1, small[4:5, :])
    gatt[...] = grad_attended
    wide[...] = grad_attended.astype(BF16)
    gsmall[3:4, :] = column_sum(wide[...].astype(F32))
    go[...] = dot_tn(ctxbuf[...], wide[...]).astype(BF16)
    gctx[...] = dot_nt(wide[...], wo[...]).astype(BF16)

    if pieces:
        n_k = len(outs) // 2
        for k in range(n_k):
            for keep in range(2):
                out = outs[2 * k + keep]
                h = half if keep else 1 - half
                col = pl.multiple_of(h * HALF, 128)
                for xx in range(2):
                    s = meta[2 * k + xx]
                    for yt in range(2):
                        t = 1 - kind if yt else kind
                        for b in range(GROUPS):
                            row = pl.multiple_of(block_row(t, s, b), 8)
                            start(
                                gf.at[pl.ds(row, block), pl.ds(col, HALF)],
                                out.at[yt, xx, pl.ds(b * block, block), :],
                                sems.at[0],
                            )
                        row = pl.multiple_of(s * d + t * (d // 2), 8)
                        start(
                            go.at[pl.ds(row, d // 2), pl.ds(col, HALF)],
                            out.at[yt, xx, pl.ds(f, d // 2), :],
                            sems.at[1],
                        )
    else:
        g_outer, g_inner, g_output = outs
        start(go, g_output, sems.at[1])
        start(gf.at[pl.ds(0, ff), :], g_outer, sems.at[0])
        for b in range(GROUPS):
            start(gf.at[pl.ds(ff + b * D, D), :], g_inner.at[:, pl.ds(b * D, D)], sems.at[0])
    wait_whole(gf, sems.at[0])
    wait_whole(go, sems.at[1])


def middle(rows, pieces, meta, length, sources, ctx_parts, tok, gout, small):
    d, f = rows
    slots = tok.shape[0]
    ff = GROUPS * D
    if pieces:
        chunk = jax.ShapeDtypeStruct((2, 2, f + d // 2, HALF), BF16)
        grads = [chunk] * 8
    else:
        grads = [
            jax.ShapeDtypeStruct((ff, D), BF16),
            jax.ShapeDtypeStruct((D, ff), BF16),
            jax.ShapeDtypeStruct((D, D), BF16),
        ]
    wide = pltpu.VMEM((slots, D), F32)
    low = pltpu.VMEM((slots, D), BF16)
    return pl.pallas_call(
        functools.partial(middle_kernel, rows, pieces, len(ctx_parts)),
        in_specs=[SM, SM] + [ANY] * len(sources) + [VM] * (len(ctx_parts) + 3),
        out_specs=[VM] * 4 + [ANY] * len(grads),
        out_shape=[
            jax.ShapeDtypeStruct((slots, D), BF16),
            jax.ShapeDtypeStruct((slots, D), F32),
            jax.ShapeDtypeStruct((slots, D), BF16),
            jax.ShapeDtypeStruct((SMALL, D), F32),
        ]
        + grads,
        scratch_shapes=[
            pltpu.VMEM((2 * ff, D), BF16),
            pltpu.VMEM((D, D), BF16),
            pltpu.VMEM((2 * ff, D), BF16),
            pltpu.VMEM((D, D), BF16),
            pltpu.VMEM((GROUPS, slots, D), BF16),
            pltpu.VMEM((GROUPS, slots, D), F32),
            wide,
            wide,
            wide,
            low,
            low,
            low,
            pltpu.SemaphoreType.DMA((2,)),
        ],
        compiler_params=params(),
        cost_estimate=cost(2 * slots * D * D * 27, 24 * 2**20),
        name="middle",
    )(meta, length, *sources, *ctx_parts, tok, gout, small)


def last_kernel(rows, pieces, parts, meta, *refs):
    d, e = rows
    wqkv, tok, rel, gatt, gsmall = refs[:5]
    groups = [refs[5 + i * parts : 5 + (i + 1) * parts] for i in range(5)]
    at = 5 + 5 * parts
    gin = refs[at]
    outs = refs[at + 1 : -5]
    gw, grel, gsm, sumbuf, sems = refs[-5:]

    def whole(group):
        return jnp.concatenate([ref[...] for ref in group], axis=1)

    deltas = [whole(group) for group in groups[:3]]
    flip = flip_matrix(rel.shape[0])
    drel = [whole(groups[4]), dot(flip, whole(groups[3])).astype(BF16)]
    sumbuf[...] = gsmall[...]
    total = gatt[...]
    embed = None
    for p in range(3):
        total = total + dot_nt(deltas[p], wqkv[p])
        part = dot_tn(tok[...], deltas[p])
        bias = column_sum(deltas[p].astype(F32))
        if p < 2:
            part = part + dot_tn(rel[...], drel[p])
            bias = bias + column_sum(drel[p].astype(F32))
            back = dot_nt(drel[p], wqkv[p])
            embed = back if embed is None else embed + back
        gw[p] = part.astype(BF16)
        sumbuf[p : p + 1, :] = bias
    gin[...] = total.astype(BF16)
    grel[...] = embed.astype(BF16)
    if pieces:
        half = meta[8]
        gsm[...] = jnp.zeros(gsm.shape, BF16)
        gsm[:, 0:128] = cut_small(sumbuf[...], d)
        n_k = len(outs) // 2
        for k in range(n_k):
            for keep in range(2):
                out = outs[2 * k + keep]
                h = half if keep else 1 - half
                col = pl.multiple_of(h * HALF, 128)
                for xx in range(2):
                    s = meta[2 * k + xx]
                    for p in range(3):
                        start(
                            gw.at[p, pl.ds(pl.multiple_of(s * d, 8), d), pl.ds(col, HALF)],
                            out.at[xx, pl.ds(p * d, d), :],
                            sems.at[0],
                        )
                    start(
                        grel.at[pl.ds(pl.multiple_of(s * e, 8), e), pl.ds(col, HALF)],
                        out.at[xx, pl.ds(3 * d, e), :],
                        sems.at[1],
                    )
                    start(
                        gsm.at[pl.ds(pl.multiple_of(s * SMALL, SMALL), SMALL), pl.ds(col, HALF)],
                        out.at[xx, pl.ds(3 * d + e, SMALL), :],
                        sems.at[2],
                    )
        wait_whole(gsm, sems.at[2])
    else:
        g_w, g_rel, g_small = outs
        start(gw, g_w, sems.at[0])
        start(grel, g_rel, sems.at[1])
        g_small[...] = sumbuf[...]
    wait_whole(gw, sems.at[0])
    wait_whole(grel, sems.at[1])


def last(rows, pieces, meta, wqkv, tok, rel, gatt, gsmall, groups):
    d, e = rows
    slots = tok.shape[0]
    parts = len(groups[0])
    if pieces:
        grads = [jax.ShapeDtypeStruct((2, 3 * d + e + SMALL, HALF), BF16)] * 8
        specs = [ANY] * 8
    else:
        grads = [
            jax.ShapeDtypeStruct((3, D, D), BF16),
            jax.ShapeDtypeStruct(rel.shape, BF16),
            jax.ShapeDtypeStruct((SMALL, D), F32),
        ]
        specs = [ANY, ANY, VM]
    flat = [ref for group in groups for ref in group]
    return pl.pallas_call(
        functools.partial(last_kernel, rows, pieces, parts),
        in_specs=[SM] + [VM] * (5 + len(flat)),
        out_specs=[VM] + specs,
        out_shape=[jax.ShapeDtypeStruct((slots, D), BF16)] + grads,
        scratch_shapes=[
            pltpu.VMEM((3, D, D), BF16),
            pltpu.VMEM(rel.shape, BF16),
            pltpu.VMEM((128, D), BF16),
            pltpu.VMEM((SMALL, D), F32),
            pltpu.SemaphoreType.DMA((3,)),
        ],
        compiler_params=params(),
        cost_estimate=cost(2 * D * D * (6 * 256 + 4 * 512), 12 * 2**20),
        name="last",
    )(meta, wqkv, tok, rel, gatt, gsmall, *flat)


def pack_small(vectors, inner, width):
    block = jnp.concatenate([v[None] for v in vectors] + [inner.reshape(GROUPS, width)], axis=0)
    block = jnp.pad(block, ((0, SMALL - block.shape[0]), (0, HALF - width)))
    return jnp.concatenate([block, block], axis=1)


def add(a, b):
    return a.astype(F32) + b.astype(F32)


def local(
    tokens,
    lengths,
    grad_output,
    w_query,
    b_query,
    w_key,
    b_key,
    w_value,
    b_value,
    w_output,
    b_output,
    first_gain,
    first_bias,
    w_inner,
    b_inner,
    w_outer,
    b_outer,
    second_gain,
    second_bias,
    relative_embed,
):
    n = lax.axis_size("mp")
    dp_size = lax.axis_size("dp")
    d, e, f = w_query.shape[0], relative_embed.shape[0], w_outer.shape[0]
    tok = tokens[0]
    vectors = (
        b_query,
        b_key,
        b_value,
        b_output,
        first_gain,
        first_bias,
        b_outer,
        second_gain,
        second_bias,
    )
    ringed = n == 8 and dp_size == 4 and d % 16 == 0
    row_share = 1.0 / (tokens.shape[0] * dp_size * n)
    split_heads = 3
    pairs = PAIRS // split_heads

    if ringed:
        depth = n // 2
        dp_at, mp_at = lax.axis_index("dp"), lax.axis_index("mp")
        core, row = dp_at % 2, dp_at // 2
        z_at, x_at = mp_at // 2, mp_at % 2
        owners = [
            ((z_at - k) % depth) * 2 + (x_at if xx == 0 else 1 - x_at)
            for k in range(depth)
            for xx in range(2)
        ]
        meta = jnp.stack(owners + [core, row]).astype(jnp.int32)
        near = [(i, i ^ 1) for i in range(dp_size)]
        side = [(i, i ^ 2) for i in range(dp_size)]
        cross = [(i, i ^ 1) for i in range(n)]
        along = [(i, (i + 2) % n) for i in range(n)]

        def to_core(v):
            return lax.ppermute(v, "dp", near)

        def to_y(v):
            return lax.ppermute(v, "dp", side)

        def to_x(v):
            return lax.ppermute(v, "mp", cross)

        def to_z(v):
            return lax.ppermute(v, "mp", along)

        own_a = jnp.concatenate(
            [w_query, w_key, w_value, relative_embed, pack_small(vectors, b_inner, d)], axis=0
        )
        half_a = lax.dynamic_slice_in_dim(own_a, core * HALF, HALF, axis=1)
        a_pieces, a_sources = [], [own_a]
        held = half_a
        for k in range(depth):
            if k:
                held = to_z(held)
            for xx in range(2):
                if k == 0 and xx == 0:
                    continue
                got = to_x(held) if xx else held
                a_pieces += [(2 * k + xx, False), (2 * k + xx, True)]
                a_sources += [got, to_core(got)]
        inner_rows = jnp.concatenate(
            [w_inner[:, g * D : (g + 1) * D] for g in range(GROUPS)] + [w_output[d // 2 :]], axis=0
        )
        outer_rows = jnp.concatenate([w_outer, w_output[: d // 2]], axis=0)
        own_f = jnp.where(row == 0, outer_rows, inner_rows)
        held = lax.dynamic_slice_in_dim(own_f, core * HALF, HALF, axis=1)
        f_pieces, f_sources = [], [w_outer, w_inner, w_output]
        for k in range(depth):
            if k:
                held = to_z(held)
            for xx in range(2):
                if k == 0 and xx == 0:
                    continue
                got = to_x(held) if xx else held
                turned = to_y(got)
                slot = 2 * k + xx
                f_pieces += [(slot, h, t) for t in (False, True) for h in (False, True)]
                f_sources += [got, to_core(got), turned, to_core(turned)]
    else:
        meta = jnp.zeros((10,), jnp.int32)

        def gathered(value):
            return lax.all_gather(value, "mp", axis=0, tiled=True)

        small_full = jnp.concatenate(
            [gathered(v)[None] for v in vectors] + [gathered(b_inner).reshape(GROUPS, D)], axis=0
        )
        small_full = jnp.pad(small_full.astype(F32), ((0, SMALL - 13), (0, 0)))
        full_w = jnp.stack([gathered(w) for w in (w_query, w_key, w_value)])
        a_pieces, a_sources = [], [full_w, gathered(relative_embed), small_full]
        f_pieces, f_sources = [], [gathered(w) for w in (w_outer, w_inner, w_output)]

    qkv, wqkv, rel, rk_rev, rq_rev, rq, small = project((d, e), a_pieces, meta, a_sources, tok)
    forward = [
        attend(lengths, qkv, rk_rev, rq_rev, i * pairs, pairs) for i in range(split_heads)
    ]
    layer, gatt, gctx, gsmall, *grads_f = middle(
        (d, f), f_pieces, meta, lengths, f_sources, [c for c, _ in forward], tok, grad_output[0], small
    )
    backward = [
        attend_back(qkv, rk_rev, rq, gctx, forward[i][1], i * pairs, pairs)
        for i in range(split_heads)
    ]
    gin, *grads_a = last(
        (d, e), a_pieces, meta, wqkv, tok, rel, gatt, gsmall, list(zip(*backward))
    )

    if ringed:
        order = list(range(1, depth)) + [0]
        total_f = None
        for k in order:
            send, keep = grads_f[2 * k], grads_f[2 * k + 1]
            both = add(keep, to_core(send)).astype(BF16)
            both = add(both[0], to_y(both[1])).astype(BF16)
            mine = add(both[0], to_x(both[1]))
            if total_f is not None:
                mine = mine + to_z(total_f).astype(F32)
            total_f = mine.astype(BF16)
        other_f = to_y(total_f)
        near_f, near_other = to_core(total_f), to_core(other_f)
        total_a = None
        for k in order:
            send, keep = grads_a[2 * k], grads_a[2 * k + 1]
            both = add(keep, to_core(send)).astype(BF16)
            mine = add(both[0], to_x(both[1]))
            if total_a is not None:
                mine = mine + to_z(total_a).astype(F32)
            total_a = mine.astype(BF16)
        total_a = add(total_a, to_y(total_a)).astype(BF16)
        near_a = to_core(total_a)

        def joined(mine, other):
            left = jnp.where(core == 0, mine, other)
            right = jnp.where(core == 0, other, mine)
            return jnp.concatenate([left, right], axis=1).astype(F32) * row_share

        mine_f, mirror_f = joined(total_f, near_f), joined(other_f, near_other)
        outer = jnp.where(row == 0, mine_f, mirror_f)
        inner = jnp.where(row == 0, mirror_f, mine_f)
        grad_w_outer = outer[:f]
        block = f // GROUPS
        grad_w_inner = jnp.concatenate(
            [inner[g * block : (g + 1) * block] for g in range(GROUPS)], axis=1
        )
        grad_w_output = jnp.concatenate([outer[f:], inner[f:]], axis=0)
        whole_a = joined(total_a, near_a)
        grad_w_query, grad_w_key, grad_w_value = (whole_a[p * d : (p + 1) * d] for p in range(3))
        grad_relative = whole_a[3 * d : 3 * d + e]
        grad_small = whole_a[3 * d + e :, :d]
        small_grads = [grad_small[i] for i in range(9)]
        grad_b_inner = grad_small[9:13].reshape(f)
    else:

        def reduced(value):
            part = lax.psum_scatter(
                value.astype(F32) * row_share, "mp", scatter_dimension=0, tiled=True
            )
            return lax.psum(part.astype(BF16), "dp").astype(F32)

        grad_w_outer, grad_w_inner, grad_w_output = (reduced(g) for g in grads_f)
        g_w, g_rel, g_small = grads_a
        grad_w_query, grad_w_key, grad_w_value = (reduced(g_w[p]) for p in range(3))
        grad_relative = reduced(g_rel)
        small_grads = [reduced(g_small[i]) for i in range(9)]
        grad_b_inner = reduced(g_small[9:13].reshape(GROUPS * D))

    (
        grad_b_query,
        grad_b_key,
        grad_b_value,
        grad_b_output,
        grad_first_gain,
        grad_first_bias,
        grad_b_outer,
        grad_second_gain,
        grad_second_bias,
    ) = small_grads
    return (
        layer[None],
        gin[None],
        grad_w_query,
        grad_b_query,
        grad_w_key,
        grad_b_key,
        grad_w_value,
        grad_b_value,
        grad_w_output,
        grad_b_output,
        grad_first_gain,
        grad_first_bias,
        grad_w_inner,
        grad_b_inner,
        grad_w_outer,
        grad_b_outer,
        grad_second_gain,
        grad_second_bias,
        grad_relative,
    )


def solution(mesh):
    rows = P(("dp", "mp"), None, None)
    matrix, vector = P("mp", None), P("mp")
    weights = (matrix, vector) * 4 + (vector, vector) + (matrix, vector) * 2 + (vector, vector)
    return jax.shard_map(
        local,
        mesh=mesh,
        in_specs=(rows, P(("dp", "mp")), rows) + weights + (matrix,),
        out_specs=(rows, rows) + weights + (matrix,),
        check_vma=False,
    )
```
